32 devices in a mesh: sec: 4 (over y, x), seq: 8 (over z, core).
Axes of the slice: x: 2, y: 2, z: 4, core: 2. Of those that a mesh axis runs over, the one named last changes fastest.
Arguments:
- long_queries: bfloat16 [16, 4096], P('sec'), may hold values from -15 to 15
- long_keys: bfloat16 [512, 16, 2048], P(('sec', 'seq')), may hold values from -6 to 6
- long_values: bfloat16 [512, 16, 2048], P(('sec', 'seq')), may hold values from -6 to 6
- page_table: int32 [16, 32], replicated, may hold values from 0 to 511, as said below
- long_lengths: int32 [16], replicated, may hold values from 1 to 512, 5120 in all
- short_queries: bfloat16 [32, 256], P(('sec', 'seq')), may hold values from -15 to 15
- short_keys: bfloat16 [32, 2048, 128], P(('sec', 'seq')), may hold values from -6 to 6
- short_values: bfloat16 [32, 2048, 128], P(('sec', 'seq')), may hold values from -6 to 6
- short_lengths: int32 [2], replicated, may hold values from 1 to 2048, 2560 in all
- out_weight: bfloat16 [4096, 4608], P('seq', 'sec'), may hold values from -0.09375 to 0.09375
- long_resid: bfloat16 [16, 4608], P(None, 'sec'), may hold values from -1.5 to 1.5
Outputs:
- long_out: bfloat16 [16, 4608], P(None, 'sec')
- short_out: bfloat16 [32, 256], P(('sec', 'seq'))
The draws below stay inside these ranges and needn't reach their ends.
Inputs may be any that keep to these rules, and one draw needn't show every extreme that they name: `page_table`: row r lists the 32 pool pages of long request r in order of position; every page of the pool of 512 appears exactly once; page g is held by device g // 16 along sec+seq. `long_lengths`: counts the newest token; later slots are unused. `short_lengths`: counts the newest token; later slots are unused.
All inputs are finite; a program needn't handle non-finite values.
Results may differ from the reference program's by a relative error of at most 0.0055.
Values may be sent and summed in bfloat16 or wider, within the bound.
A program may use at most 64 MiB of HBM per device.

```python
import math
import jax
import jax.numpy as jnp
import numpy as np
from jax import lax

D = 4608
H = 32
KVH = 16
HD = 128
G = 2
RL = 16
PAGE = 16
LS = 2048
POOL = 512
PPR = 32
LMAX = 512
RS = 2


def draw_page_table(key, part):
    order = jax.random.permutation(jax.random.fold_in(key, 11), POOL)
    return order.reshape(RL, PPR).astype(jnp.int32)


def shard_levels(own_key, dims, pieces, low, high):
    def one(axis_at, shards_of):
        heights = jax.random.uniform(jax.random.fold_in(jax.random.fold_in(own_key, 6), axis_at), (shards_of,), jnp.float32, low / len(pieces), high / len(pieces))
        return jnp.repeat(jnp.exp(heights), dims[axis_at] // shards_of).reshape((-1,) + (1,) * (len(dims) - axis_at - 1))

    factor_of = one(*pieces[0])
    for cut in pieces[1:]:
        factor_of = factor_of * one(*cut)
    return factor_of


def split_up(count, total, reach, slope):
    loads = [(1 << 20) // math.isqrt(grade ** slope) + 1 for grade in range(2, count + 1)]
    rest, counts = total - reach - (count - 1), [1] * (count - 1)
    while rest > 0:
        candidates = [i for i in range(count - 1) if counts[i] < reach]
        whole, budget = sum([loads[i] for i in candidates]), rest
        for i in candidates:
            more = min(reach - counts[i], max(1, budget * loads[i] // whole), rest)
            counts[i] = counts[i] + more
            rest = rest - more
    return np.array([reach] + counts)


def uneven(stream_key, amount, total, reach, lean):
    if amount == 2:
        one = jax.random.randint(stream_key, (), max(1, total - reach), min(reach, total - 1) + 1)
        return jnp.stack([one, total - one])
    sizes = jnp.asarray(split_up(amount, total, reach, lean), jnp.int32)
    couples = (amount - 1) // 2
    donor, taker = sizes[1:1 + 2 * couples:2], sizes[2:2 + 2 * couples:2]
    slack = jnp.minimum(donor - 1, reach - taker)
    moved = jax.random.randint(jax.random.fold_in(stream_key, 1), (couples,), 0, 1 << 20) % (slack + 1)
    sizes = sizes.at[1:1 + 2 * couples:2].set(donor - moved).at[2:2 + 2 * couples:2].set(taker + moved)
    return sizes[jax.random.permutation(jax.random.fold_in(stream_key, 2), amount)]


def centred(own_key, extent, deviation, limit, cuts=(), kind=jnp.bfloat16):
    gain = shard_levels(own_key, extent, cuts, -0.22, 0.18) if cuts else 1.0
    values = jax.random.normal(own_key, extent, jnp.float32) * deviation * gain
    return jnp.minimum(jnp.maximum(values, -limit), limit).astype(kind)


def setup_inputs(seed: int = 0) -> dict:
    keys = jax.random.split(jax.random.key(seed), 12)
    long_queries = centred(keys[0], (RL, H * HD), 2.5, 15.0, ((0, 4),))
    long_keys = centred(keys[1], (POOL, PAGE, KVH * HD), 1.0, 6.0, ((0, 32),))
    long_values = centred(keys[2], (POOL, PAGE, KVH * HD), 1.0, 6.0, ((0, 32),))
    page_table = draw_page_table(jax.random.fold_in(keys[11], 71), 0)
    long_lengths = uneven(keys[4], RL, RL * LMAX * 5 // 8, LMAX, 2).astype(jnp.int32)
    short_queries = centred(keys[5], (RS * KVH, G * HD), 2.5, 15.0, ((0, 32),))
    short_keys = centred(keys[6], (RS * KVH, LS, HD), 1.0, 6.0, ((0, 32),))
    short_values = centred(keys[7], (RS * KVH, LS, HD), 1.0, 6.0, ((0, 32),))
    short_lengths = uneven(keys[8], RS, RS * LS * 5 // 8, LS, 2).astype(jnp.int32)
    out_weight = centred(keys[9], (H * HD, D), (H * HD) ** -0.5, 0.09375, ((0, 8), (1, 4)))
    long_resid = centred(keys[10], (RL, D), 0.25, 1.5, ((1, 4),))
    return dict(long_queries=long_queries, long_keys=long_keys, long_values=long_values, page_table=page_table, long_lengths=long_lengths, short_queries=short_queries, short_keys=short_keys, short_values=short_values, short_lengths=short_lengths, out_weight=out_weight, long_resid=long_resid)


soft_cap = 50.0
score_scale = 144.0 ** -0.5


def capped_weights(raw_scores, live_mask):
    capped = soft_cap * jnp.tanh(raw_scores * (score_scale / soft_cap))
    return jnp.where(live_mask, jnp.exp(capped), 0.0)


def reference(long_queries, long_keys, long_values, page_table, long_lengths, short_queries, short_keys, short_values, short_lengths, out_weight, long_resid):
    def one_request(index):
        page_rows = page_table[index]
        key_rows = long_keys[page_rows].reshape(LMAX, KVH, HD).astype(jnp.float32)
        value_rows = long_values[page_rows].reshape(LMAX, KVH, HD).astype(jnp.float32)
        query = long_queries[index].reshape(KVH, G, HD).astype(jnp.float32)
        raw_scores = jnp.einsum("hgd,thd->hgt", query, key_rows, precision=lax.Precision.HIGHEST)
        live_mask = jnp.arange(LMAX, dtype=jnp.int32) < long_lengths[index]
        weights = capped_weights(raw_scores, live_mask[None, None, :])
        totals = jnp.sum(weights, axis=2)
        rounded = weights.astype(jnp.bfloat16).astype(jnp.float32)
        part_sums = jnp.einsum("hgt,thd->hgd", rounded, value_rows, precision=lax.Precision.HIGHEST)
        return (part_sums / totals[:, :, None]).astype(jnp.bfloat16).reshape(H * HD)

    attention = lax.map(one_request, jnp.arange(RL, dtype=jnp.int32))
    projected = jnp.dot(attention, out_weight, preferred_element_type=jnp.float32)
    long_out = (long_resid.astype(jnp.float32) + projected).astype(jnp.bfloat16)

    def one_short(items):
        query_rows, key_rows, value_rows, limit_now = items
        query_rows = query_rows.reshape(KVH, G, HD).astype(jnp.float32)
        raw_scores = jnp.einsum("hgd,htd->hgt", query_rows, key_rows.astype(jnp.float32), precision=lax.Precision.HIGHEST)
        live_mask = jnp.arange(LS, dtype=jnp.int32) < limit_now
        weights = capped_weights(raw_scores, live_mask[None, None, :])
        totals = jnp.sum(weights, axis=2)
        rounded = weights.astype(jnp.bfloat16).astype(jnp.float32)
        part_sums = jnp.einsum("hgt,htd->hgd", rounded, value_rows.astype(jnp.float32), precision=lax.Precision.HIGHEST)
        return (part_sums / totals[:, :, None]).astype(jnp.bfloat16).reshape(KVH, G * HD)

    short_all = lax.map(one_short, (short_queries.reshape(RS, KVH, G * HD), short_keys.reshape(RS, KVH, LS, HD), short_values.reshape(RS, KVH, LS, HD), short_lengths))
    short_out = short_all.reshape(RS * KVH, G * HD)
    return (long_out, short_out)
```

```python
import functools
import jax
import jax.numpy as jnp
from jax import lax
from jax.experimental import pallas as pl
from jax.experimental.pallas import tpu as pltpu
from jax.sharding import PartitionSpec as P

KVH = 16
HD = 128
G = 2


soft_cap = 50.0
score_scale = 144.0 ** (-0.5)


def capped_weights(raw_scores, live_mask):
    capped = soft_cap * jnp.tanh(raw_scores * (score_scale / soft_cap))
    return jnp.where(live_mask, jnp.exp(capped), 0.0)


def per_device(
    long_queries,
    long_keys,
    long_values,
    page_table,
    long_lengths,
    short_queries,
    short_keys,
    short_values,
    short_lengths,
    out_weight,
    long_resid,
):
    queries = lax.all_gather(long_queries, "sec", axis=0, tiled=True)
    requests = queries.shape[0]
    page_count, page_len, kv_width = long_keys.shape
    tokens = page_count * page_len
    head_count = KVH * G
    first_page = lax.axis_index(("sec", "seq")) * page_count
    page_ids = first_page + jnp.arange(page_count, dtype=jnp.int32)
    matched = page_table[:, :, None] == page_ids[None, None, :]
    page_held = jnp.any(matched, axis=1)
    slot_index = jnp.arange(page_table.shape[1], dtype=jnp.int32)
    slot_of = jnp.sum(jnp.where(matched, slot_index[None, :, None], 0), axis=1)
    position = slot_of[:, :, None] * page_len + jnp.arange(page_len, dtype=jnp.int32)[None, None, :]
    live_mask = page_held[:, :, None] & (position < long_lengths[:, None, None])
    live_mask = live_mask.reshape(requests, tokens)
    grouped = (
        queries.reshape(requests, KVH, G, HD).transpose(1, 0, 2, 3).reshape(KVH, requests * G, HD)
    )
    key_rows = long_keys.reshape(tokens, KVH, HD)
    value_rows = long_values.reshape(tokens, KVH, HD)
    raw_scores = jnp.einsum("hqd,thd->hqt", grouped, key_rows, preferred_element_type=jnp.float32)
    token_mask = jnp.broadcast_to(live_mask[None, :, None, :], (KVH, requests, G, tokens)).reshape(
        KVH, requests * G, tokens
    )
    weights = capped_weights(raw_scores, token_mask)
    totals = jnp.sum(weights, axis=2)
    part_sums = jnp.einsum(
        "hqt,thd->hqd", weights.astype(jnp.bfloat16), value_rows, preferred_element_type=jnp.float32
    )
    part_sums = (
        part_sums.reshape(KVH, requests, G, HD)
        .transpose(1, 0, 2, 3)
        .reshape(requests, head_count * HD)
    )
    totals = totals.reshape(KVH, requests, G).transpose(1, 0, 2).reshape(requests, head_count)
    share_width = out_weight.shape[0]
    share_start = lax.axis_index("seq") * share_width
    part_sums, totals = lax.psum((part_sums, totals), ("sec", "seq"))
    attention = (
        (part_sums.reshape(requests, head_count, HD) / totals[:, :, None])
        .astype(jnp.bfloat16)
        .reshape(requests, head_count * HD)
    )
    feature_rows = lax.dynamic_slice_in_dim(attention, share_start, share_width, 1)
    partial_proj = jnp.dot(feature_rows, out_weight, preferred_element_type=jnp.float32)
    projected = lax.psum(partial_proj, "seq")
    long_out = (long_resid.astype(jnp.float32) + projected).astype(jnp.bfloat16)
    pair_count = short_queries.shape[0]
    length = short_keys.shape[1]
    pair_ids = lax.axis_index(("sec", "seq")) * pair_count + jnp.arange(pair_count, dtype=jnp.int32)
    request_of = pair_ids // KVH
    chosen = request_of[:, None] == jnp.arange(short_lengths.shape[0], dtype=jnp.int32)[None, :]
    pair_limit = jnp.sum(jnp.where(chosen, short_lengths[None, :], 0), axis=1)
    short_live = jnp.arange(length, dtype=jnp.int32)[None, :] < pair_limit[:, None]
    pair_queries = short_queries.reshape(pair_count, G, HD)
    short_scores = jnp.einsum(
        "pgd,ptd->pgt", pair_queries, short_keys, preferred_element_type=jnp.float32
    )
    short_weights = capped_weights(short_scores, short_live[:, None, :])
    short_totals = jnp.sum(short_weights, axis=2)
    short_sums = jnp.einsum(
        "pgt,ptd->pgd",
        short_weights.astype(jnp.bfloat16),
        short_values,
        preferred_element_type=jnp.float32,
    )
    short_out = (
        (short_sums / short_totals[:, :, None]).astype(jnp.bfloat16).reshape(pair_count, G * HD)
    )
    return (long_out, short_out)


MESH = pl.DeviceIdType.MESH
CONTRACT_LAST = (((1,), (1,)), ((), ()))


def decode_kernel(
    n_sec,
    n_seq,
    page_len,
    q_ref,
    k_hbm,
    v_hbm,
    table_ref,
    lens_ref,
    sq_ref,
    sk_hbm,
    sv_hbm,
    slens_ref,
    w_hbm,
    resid_ref,
    long_ref,
    short_ref,
    k_ref,
    v_ref,
    sk_ref,
    sv_ref,
    w_ref,
    q_slabs,
    q_rows,
    mask_ref,
    part_send,
    part_recv,
    part_own,
    sec_buf,
    pair_send,
    pair_recv,
    z_buf,
    fin_buf,
    load_sem,
    q_send_sem,
    q_recv_sem,
    a_send_sem,
    a_recv_sem,
    b_send_sem,
    b_recv_sem,
    c_send_sem,
    c_recv_sem,
    z_send_sem,
    z_recv_sem,
    f_send_sem,
    f_recv_sem,
):
    sec = lax.axis_index("sec")
    seq = lax.axis_index("seq")
    core = lax.rem(seq, 2)
    deep = seq // 2
    n_deep = n_seq // 2
    mate = seq + 1 - 2 * core
    sec_peers = [lax.rem(sec + i, n_sec) for i in range(1, n_sec)]
    seq_peers = [lax.rem(seq + i, n_seq) for i in range(1, n_seq)]

    barrier = pltpu.get_barrier_semaphore()
    for peer in sec_peers:
        pl.semaphore_signal(barrier, inc=1, device_id={"sec": peer}, device_id_type=MESH)
    for peer in seq_peers:
        pl.semaphore_signal(barrier, inc=1, device_id={"seq": peer}, device_id_type=MESH)

    loads = []
    for i, (src, dst) in enumerate(
        (
            (q_ref, q_slabs.at[sec]),
            (sk_hbm, sk_ref),
            (sv_hbm, sv_ref),
            (k_hbm, k_ref),
            (v_hbm, v_ref),
            (w_hbm, w_ref),
        )
    ):
        copy = pltpu.make_async_copy(src, dst, load_sem.at[i])
        copy.start()
        loads.append(copy)

    slab_rows = q_ref.shape[0]
    requests, slots = table_ref.shape
    tokens = k_ref.shape[0]
    page_count = tokens // page_len
    first_page = (sec * n_seq + seq) * page_count
    token = lax.broadcasted_iota(jnp.int32, (requests, tokens), 1)
    row = lax.broadcasted_iota(jnp.int32, (requests, tokens), 0)
    page_of = first_page + token // page_len
    slot_of = jnp.full((requests, tokens), 1 << 20, jnp.int32)
    table = table_ref[...]
    for s in range(slots):
        slot_of = jnp.where(table[:, s : s + 1] == page_of, s, slot_of)
    limits = jnp.zeros((requests, tokens), jnp.int32)
    for r in range(requests):
        limits = jnp.where(row == r, lens_ref[r], limits)
    position = slot_of * page_len + lax.rem(token, page_len)
    live = jnp.where(position < limits, 1.0, 0.0).astype(jnp.float32)
    for g in range(G):
        mask_ref[g * requests : (g + 1) * requests, :] = live

    pl.semaphore_wait(barrier, n_sec + n_seq - 2)
    loads[0].wait()
    q_copies = []
    for i, peer in enumerate(sec_peers):
        copy = pltpu.make_async_remote_copy(
            src_ref=q_ref,
            dst_ref=q_slabs.at[sec],
            send_sem=q_send_sem.at[i],
            recv_sem=q_recv_sem.at[sec],
            device_id={"sec": peer},
            device_id_type=MESH,
        )
        copy.start()
        q_copies.append(copy)

    factor = score_scale / soft_cap
    loads[1].wait()
    loads[2].wait()
    pair_count = sq_ref.shape[0]
    length = sk_ref.shape[0] // pair_count
    short_at = lax.broadcasted_iota(jnp.int32, (8, length), 1)
    which = lax.broadcasted_iota(jnp.int32, (8, HD), 0)
    for p in range(pair_count):
        pair_id = (sec * n_seq + seq) * pair_count + p
        limit = slens_ref[pair_id // KVH]
        q_pair = sq_ref[p : p + 1, :].astype(jnp.float32)
        stacked = jnp.zeros((8, HD), jnp.float32)
        for g in range(G):
            stacked = jnp.where(which == g, q_pair[:, g * HD : (g + 1) * HD], stacked)
        raw = lax.dot_general(
            stacked.astype(jnp.bfloat16),
            sk_ref[p * length : (p + 1) * length, :],
            CONTRACT_LAST,
            preferred_element_type=jnp.float32,
        )
        weights = jnp.where(short_at < limit, jnp.exp(soft_cap * jnp.tanh(raw * factor)), 0.0)
        totals = jnp.sum(weights, axis=1, keepdims=True)
        sums = jnp.dot(
            weights.astype(jnp.bfloat16),
            sv_ref[p * length : (p + 1) * length, :],
            preferred_element_type=jnp.float32,
        )
        result = (sums / totals).astype(short_ref.dtype)
        for g in range(G):
            short_ref[p : p + 1, g * HD : (g + 1) * HD] = result[g : g + 1, :]

    loads[3].wait()
    loads[4].wait()
    for i, peer in enumerate(sec_peers):
        pltpu.make_async_remote_copy(
            src_ref=q_ref,
            dst_ref=q_slabs.at[peer],
            send_sem=q_send_sem.at[i],
            recv_sem=q_recv_sem.at[peer],
            device_id={"sec": peer},
            device_id_type=MESH,
        ).wait_recv()
    for s in range(n_sec):
        q_rows[s * slab_rows : (s + 1) * slab_rows, :] = q_slabs[s].astype(jnp.float32)

    share = w_ref.shape[0]
    heads = share // (G * HD)
    blocks = share // HD
    lane = lax.broadcasted_iota(jnp.int32, (requests, HD), 1)
    a_copies = []
    half = n_seq // 2
    order = [half]
    for i in range(1, half):
        order += [half + i, half - i]
    order.append(0)
    mask = mask_ref[...]
    for step, offset in enumerate(order):
        dest = lax.rem(seq + offset, n_seq) if offset else seq
        total_block = jnp.zeros((requests, HD), jnp.float32)
        for a in range(heads):
            at = pl.multiple_of(dest * share + a * G * HD, G * HD)
            kv_at = pl.multiple_of((dest * heads + a) * HD, HD)
            q_now = jnp.concatenate(
                [q_rows[:, pl.ds(pl.multiple_of(at + g * HD, HD), HD)] for g in range(G)], axis=0
            ).astype(jnp.bfloat16)
            raw = lax.dot_general(
                q_now,
                k_ref[:, pl.ds(kv_at, HD)],
                CONTRACT_LAST,
                preferred_element_type=jnp.float32,
            )
            weights = jnp.exp(soft_cap * jnp.tanh(raw * factor)) * mask
            totals = jnp.sum(weights, axis=1, keepdims=True)
            sums = jnp.dot(
                weights.astype(jnp.bfloat16),
                v_ref[:, pl.ds(kv_at, HD)],
                preferred_element_type=jnp.float32,
            )
            for g in range(G):
                b = a * G + g
                piece = sums[g * requests : (g + 1) * requests, :]
                total = totals[g * requests : (g + 1) * requests, :]
                total_block = jnp.where(lax.rem(lane, blocks) == b, total, total_block)
                if offset:
                    part_send[step, :, b * HD : (b + 1) * HD] = piece.astype(jnp.bfloat16)
                else:
                    part_own[:, b * HD : (b + 1) * HD] = piece
        if offset:
            high = total_block.astype(jnp.bfloat16)
            low = (total_block - high.astype(jnp.float32)).astype(jnp.bfloat16)
            part_send[step, :, share : share + HD] = jnp.where(
                lane < blocks, high.astype(jnp.float32), low.astype(jnp.float32)
            ).astype(jnp.bfloat16)
            copy = pltpu.make_async_remote_copy(
                src_ref=part_send.at[step],
                dst_ref=part_recv.at[n_seq - offset],
                send_sem=a_send_sem.at[step],
                recv_sem=a_recv_sem.at[n_seq - offset],
                device_id={"seq": dest},
                device_id_type=MESH,
            )
            copy.start()
            a_copies.append(copy)
        else:
            part_own[:, share : share + HD] = jnp.where(lane < blocks, total_block, 0.0)

    gathered = part_own[...]
    for copy, offset in zip(a_copies, order):
        pltpu.make_async_remote_copy(
            src_ref=part_send.at[0],
            dst_ref=part_recv.at[offset],
            send_sem=a_send_sem.at[0],
            recv_sem=a_recv_sem.at[offset],
            device_id={"seq": seq_peers[0]},
            device_id_type=MESH,
        ).wait_recv()
        gathered = gathered + part_recv[offset].astype(jnp.float32)

    totals_part = gathered[:, share : share + HD]
    totals_part = totals_part + pltpu.roll(totals_part, HD - blocks, 1)
    repeated = totals_part
    for i in range(1, 2):
        repeated = jnp.where(lane < blocks, repeated, pltpu.roll(totals_part, blocks, 1))
    high = repeated.astype(jnp.bfloat16).astype(jnp.float32)
    tail_block = jnp.where(lane < blocks, high, repeated - high)
    sec_buf[0, :, 0:share] = gathered[:, 0:share].astype(jnp.bfloat16)
    sec_buf[0, :, share : share + HD] = tail_block.astype(jnp.bfloat16)
    b_copies = []
    for i, peer in enumerate(sec_peers):
        copy = pltpu.make_async_remote_copy(
            src_ref=sec_buf.at[0],
            dst_ref=sec_buf.at[n_sec - 1 - i],
            send_sem=b_send_sem.at[i],
            recv_sem=b_recv_sem.at[n_sec - 1 - i],
            device_id={"sec": peer},
            device_id_type=MESH,
        )
        copy.start()
        b_copies.append(copy)
    sums_now = gathered[:, 0:share]
    totals_now = jnp.where(lane < blocks, totals_part, 0.0)
    loads[5].wait()
    for i in range(1, n_sec):
        pltpu.make_async_remote_copy(
            src_ref=sec_buf.at[0],
            dst_ref=sec_buf.at[i],
            send_sem=b_send_sem.at[0],
            recv_sem=b_recv_sem.at[i],
            device_id={"sec": sec_peers[0]},
            device_id_type=MESH,
        ).wait_recv()
        arrived = sec_buf[i].astype(jnp.float32)
        sums_now = sums_now + arrived[:, 0:share]
        totals_now = totals_now + arrived[:, share : share + HD]
    totals_now = totals_now + pltpu.roll(totals_now, HD - blocks, 1)
    attention = jnp.concatenate(
        [sums_now[:, b * HD : (b + 1) * HD] / totals_now[:, b : b + 1] for b in range(blocks)],
        axis=1,
    ).astype(jnp.bfloat16)
    partial = jnp.dot(attention, w_ref[...], preferred_element_type=jnp.float32)

    rows = requests // 2
    upper, lower = partial[:rows, :], partial[rows:, :]
    first = core == 0
    pair_send[...] = jnp.where(first, lower, upper).astype(jnp.bfloat16)
    c_copy = pltpu.make_async_remote_copy(
        src_ref=pair_send,
        dst_ref=pair_recv,
        send_sem=c_send_sem,
        recv_sem=c_recv_sem,
        device_id={"seq": mate},
        device_id_type=MESH,
    )
    c_copy.start()
    mine = jnp.where(first, upper, lower)
    resid = resid_ref[...].astype(jnp.float32)
    resid = jnp.where(first, resid[:rows, :], resid[rows:, :])
    c_copy.wait_recv()
    z_buf[deep] = (mine + pair_recv[...].astype(jnp.float32)).astype(jnp.bfloat16)
    z_copies = []
    for i in range(1, n_deep):
        peer = lax.rem(deep + i, n_deep)
        copy = pltpu.make_async_remote_copy(
            src_ref=z_buf.at[deep],
            dst_ref=z_buf.at[deep],
            send_sem=z_send_sem.at[i - 1],
            recv_sem=z_recv_sem.at[deep],
            device_id={"seq": peer * 2 + core},
            device_id_type=MESH,
        )
        copy.start()
        z_copies.append(copy)
    for i in range(1, n_deep):
        peer = lax.rem(deep + i, n_deep)
        pltpu.make_async_remote_copy(
            src_ref=z_buf.at[peer],
            dst_ref=z_buf.at[peer],
            send_sem=z_send_sem.at[i - 1],
            recv_sem=z_recv_sem.at[peer],
            device_id={"seq": peer * 2 + core},
            device_id_type=MESH,
        ).wait_recv()
    for i in range(n_deep):
        resid = resid + z_buf[i].astype(jnp.float32)
    fin_buf[core] = resid.astype(jnp.bfloat16)
    f_copy = pltpu.make_async_remote_copy(
        src_ref=fin_buf.at[core],
        dst_ref=fin_buf.at[core],
        send_sem=f_send_sem,
        recv_sem=f_recv_sem,
        device_id={"seq": mate},
        device_id_type=MESH,
    )
    f_copy.start()
    for copy in q_copies + a_copies + b_copies + [c_copy] + z_copies:
        copy.wait_send()
    f_copy.wait()
    for i in range(2):
        long_ref[i * rows : (i + 1) * rows, :] = fin_buf[i]


def per_device_fused(n_sec, n_seq, *args):
    (
        long_queries,
        long_keys,
        long_values,
        page_table,
        long_lengths,
        short_queries,
        short_keys,
        short_values,
        short_lengths,
        out_weight,
        long_resid,
    ) = args
    page_count, page_len, kv_width = long_keys.shape
    tokens = page_count * page_len
    pair_count, length, _ = short_keys.shape
    slab, q_width = long_queries.shape
    requests = slab * n_sec
    share, columns = out_weight.shape
    rows = requests // 2
    packed = share + HD
    bf16, f32 = jnp.bfloat16, jnp.float32
    vmem = pl.BlockSpec(memory_space=pltpu.VMEM)
    smem = pl.BlockSpec(memory_space=pltpu.SMEM)
    hbm = pl.BlockSpec(memory_space=pltpu.HBM)
    dma = pltpu.SemaphoreType.DMA
    return pl.pallas_call(
        functools.partial(decode_kernel, n_sec, n_seq, page_len),
        out_shape=(
            jax.ShapeDtypeStruct(long_resid.shape, bf16),
            jax.ShapeDtypeStruct(short_queries.shape, bf16),
        ),
        in_specs=[vmem, hbm, hbm, vmem, smem, vmem, hbm, hbm, smem, hbm, vmem],
        out_specs=(vmem, vmem),
        scratch_shapes=[
            pltpu.VMEM((tokens, kv_width), bf16),
            pltpu.VMEM((tokens, kv_width), bf16),
            pltpu.VMEM((pair_count * length, HD), bf16),
            pltpu.VMEM((pair_count * length, HD), bf16),
            pltpu.VMEM((share, columns), bf16),
            pltpu.VMEM((n_sec, slab, q_width), bf16),
            pltpu.VMEM((requests, q_width), f32),
            pltpu.VMEM((G * requests, tokens), f32),
            pltpu.VMEM((n_seq, requests, packed), bf16),
            pltpu.VMEM((n_seq, requests, packed), bf16),
            pltpu.VMEM((requests, packed), f32),
            pltpu.VMEM((n_sec, requests, packed), bf16),
            pltpu.VMEM((rows, columns), bf16),
            pltpu.VMEM((rows, columns), bf16),
            pltpu.VMEM((n_seq // 2, rows, columns), bf16),
            pltpu.VMEM((2, rows, columns), bf16),
            dma((6,)),
            dma((n_sec,)),
            dma((n_sec,)),
            dma((n_seq,)),
            dma((n_seq,)),
            dma((n_sec,)),
            dma((n_sec,)),
            dma,
            dma,
            dma((n_seq // 2,)),
            dma((n_seq // 2,)),
            dma,
            dma,
        ],
        compiler_params=pltpu.CompilerParams(collective_id=0, has_side_effects=True),
    )(
        long_queries,
        long_keys.reshape(tokens, kv_width),
        long_values.reshape(tokens, kv_width),
        page_table,
        long_lengths,
        short_queries,
        short_keys.reshape(pair_count * length, HD),
        short_values.reshape(pair_count * length, HD),
        short_lengths,
        out_weight,
        long_resid,
    )


def pick_body(n_sec, n_seq, *args):
    share = args[9].shape[0]
    requests = args[0].shape[0] * n_sec
    if share % (G * HD) == 0 and n_seq % 2 == 0 and requests % 16 == 0:
        return per_device_fused(n_sec, n_seq, *args)
    return per_device(*args)


def solution(mesh):
    in_specs = (
        P("sec", None),
        P(("sec", "seq"), None, None),
        P(("sec", "seq"), None, None),
        P(),
        P(),
        P(("sec", "seq"), None),
        P(("sec", "seq"), None, None),
        P(("sec", "seq"), None, None),
        P(),
        P("seq", "sec"),
        P(None, "sec"),
    )
    out_specs = (P(None, "sec"), P(("sec", "seq"), None))
    body = functools.partial(pick_body, mesh.shape["sec"], mesh.shape["seq"])
    return jax.shard_map(
        body, mesh=mesh, in_specs=in_specs, out_specs=out_specs, check_vma=False
    )
```

```python
import functools
import jax
import jax.numpy as jnp
from jax import lax
from jax.experimental import pallas as pl
from jax.experimental.pallas import tpu as pltpu
from jax.sharding import PartitionSpec as P

KVH = 16
HD = 128
G = 2


soft_cap = 50.0
score_scale = 144.0 ** (-0.5)


def capped_weights(raw_scores, live_mask):
    capped = soft_cap * jnp.tanh(raw_scores * (score_scale / soft_cap))
    return jnp.where(live_mask, jnp.exp(capped), 0.0)


def per_device(
    long_queries,
    long_keys,
    long_values,
    page_table,
    long_lengths,
    short_queries,
    short_keys,
    short_values,
    short_lengths,
    out_weight,
    long_resid,
):
    queries = lax.all_gather(long_queries, "sec", axis=0, tiled=True)
    requests = queries.shape[0]
    page_count, page_len, kv_width = long_keys.shape
    tokens = page_count * page_len
    head_count = KVH * G
    first_page = lax.axis_index(("sec", "seq")) * page_count
    page_ids = first_page + jnp.arange(page_count, dtype=jnp.int32)
    matched = page_table[:, :, None] == page_ids[None, None, :]
    page_held = jnp.any(matched, axis=1)
    slot_index = jnp.arange(page_table.shape[1], dtype=jnp.int32)
    slot_of = jnp.sum(jnp.where(matched, slot_index[None, :, None], 0), axis=1)
    position = slot_of[:, :, None] * page_len + jnp.arange(page_len, dtype=jnp.int32)[None, None, :]
    live_mask = page_held[:, :, None] & (position < long_lengths[:, None, None])
    live_mask = live_mask.reshape(requests, tokens)
    grouped = (
        queries.reshape(requests, KVH, G, HD).transpose(1, 0, 2, 3).reshape(KVH, requests * G, HD)
    )
    key_rows = long_keys.reshape(tokens, KVH, HD)
    value_rows = long_values.reshape(tokens, KVH, HD)
    raw_scores = jnp.einsum("hqd,thd->hqt", grouped, key_rows, preferred_element_type=jnp.float32)
    token_mask = jnp.broadcast_to(live_mask[None, :, None, :], (KVH, requests, G, tokens)).reshape(
        KVH, requests * G, tokens
    )
    weights = capped_weights(raw_scores, token_mask)
    totals = jnp.sum(weights, axis=2)
    part_sums = jnp.einsum(
        "hqt,thd->hqd", weights.astype(jnp.bfloat16), value_rows, preferred_element_type=jnp.float32
    )
    part_sums = (
        part_sums.reshape(KVH, requests, G, HD)
        .transpose(1, 0, 2, 3)
        .reshape(requests, head_count * HD)
    )
    totals = totals.reshape(KVH, requests, G).transpose(1, 0, 2).reshape(requests, head_count)
    share_width = out_weight.shape[0]
    share_start = lax.axis_index("seq") * share_width
    part_sums, totals = lax.psum((part_sums, totals), ("sec", "seq"))
    attention = (
        (part_sums.reshape(requests, head_count, HD) / totals[:, :, None])
        .astype(jnp.bfloat16)
        .reshape(requests, head_count * HD)
    )
    feature_rows = lax.dynamic_slice_in_dim(attention, share_start, share_width, 1)
    partial_proj = jnp.dot(feature_rows, out_weight, preferred_element_type=jnp.float32)
    projected = lax.psum(partial_proj, "seq")
    long_out = (long_resid.astype(jnp.float32) + projected).astype(jnp.bfloat16)
    pair_count = short_queries.shape[0]
    length = short_keys.shape[1]
    pair_ids = lax.axis_index(("sec", "seq")) * pair_count + jnp.arange(pair_count, dtype=jnp.int32)
    request_of = pair_ids // KVH
    chosen = request_of[:, None] == jnp.arange(short_lengths.shape[0], dtype=jnp.int32)[None, :]
    pair_limit = jnp.sum(jnp.where(chosen, short_lengths[None, :], 0), axis=1)
    short_live = jnp.arange(length, dtype=jnp.int32)[None, :] < pair_limit[:, None]
    pair_queries = short_queries.reshape(pair_count, G, HD)
    short_scores = jnp.einsum(
        "pgd,ptd->pgt", pair_queries, short_keys, preferred_element_type=jnp.float32
    )
    short_weights = capped_weights(short_scores, short_live[:, None, :])
    short_totals = jnp.sum(short_weights, axis=2)
    short_sums = jnp.einsum(
        "pgt,ptd->pgd",
        short_weights.astype(jnp.bfloat16),
        short_values,
        preferred_element_type=jnp.float32,
    )
    short_out = (
        (short_sums / short_totals[:, :, None]).astype(jnp.bfloat16).reshape(pair_count, G * HD)
    )
    return (long_out, short_out)


MESH = pl.DeviceIdType.MESH
CONTRACT_LAST = (((1,), (1,)), ((), ()))


def decode_kernel(
    n_sec,
    n_seq,
    page_len,
    q_ref,
    k_hbm,
    v_hbm,
    table_ref,
    lens_ref,
    sq_ref,
    sk_hbm,
    sv_hbm,
    slens_ref,
    w_hbm,
    resid_ref,
    long_ref,
    short_ref,
    k_ref,
    v_ref,
    sk_ref,
    sv_ref,
    w_ref,
    q_slabs,
    q_rows,
    mask_ref,
    part_send,
    part_recv,
    part_own,
    sec_buf,
    pair_send,
    pair_recv,
    z_buf,
    fin_buf,
    load_sem,
    q_send_sem,
    q_recv_sem,
    a_send_sem,
    a_recv_sem,
    b_send_sem,
    b_recv_sem,
    c_send_sem,
    c_recv_sem,
    z_send_sem,
    z_recv_sem,
    f_send_sem,
    f_recv_sem,
):
    sec = lax.axis_index("sec")
    seq = lax.axis_index("seq")
    core = lax.rem(seq, 2)
    deep = seq // 2
    n_deep = n_seq // 2
    mate = seq + 1 - 2 * core
    sec_peers = [lax.rem(sec + i, n_sec) for i in range(1, n_sec)]
    seq_peers = [lax.rem(seq + i, n_seq) for i in range(1, n_seq)]

    barrier = pltpu.get_barrier_semaphore()
    for peer in sec_peers:
        pl.semaphore_signal(barrier, inc=1, device_id={"sec": peer}, device_id_type=MESH)
    for peer in seq_peers:
        pl.semaphore_signal(barrier, inc=1, device_id={"seq": peer}, device_id_type=MESH)

    loads = []
    for i, (src, dst) in enumerate(
        (
            (q_ref, q_slabs.at[sec]),
            (sk_hbm, sk_ref),
            (sv_hbm, sv_ref),
            (k_hbm, k_ref),
            (v_hbm, v_ref),
            (w_hbm, w_ref),
        )
    ):
        copy = pltpu.make_async_copy(src, dst, load_sem.at[i])
        copy.start()
        loads.append(copy)

    slab_rows = q_ref.shape[0]
    requests, slots = table_ref.shape
    tokens = k_ref.shape[0]
    page_count = tokens // page_len
    first_page = (sec * n_seq + seq) * page_count
    token = lax.broadcasted_iota(jnp.int32, (requests, tokens), 1)
    row = lax.broadcasted_iota(jnp.int32, (requests, tokens), 0)
    page_of = first_page + token // page_len
    slot_of = jnp.full((requests, tokens), 1 << 20, jnp.int32)
    table = table_ref[...]
    for s in range(slots):
        slot_of = jnp.where(table[:, s : s + 1] == page_of, s, slot_of)
    limits = jnp.zeros((requests, tokens), jnp.int32)
    for r in range(requests):
        limits = jnp.where(row == r, lens_ref[r], limits)
    position = slot_of * page_len + lax.rem(token, page_len)
    live = jnp.where(position < limits, 1.0, 0.0).astype(jnp.float32)
    for g in range(G):
        mask_ref[g * requests : (g + 1) * requests, :] = live

    pl.semaphore_wait(barrier, n_sec + n_seq - 2)
    q_copies = []
    for i, peer in enumerate(sec_peers):
        copy = pltpu.make_async_remote_copy(
            src_ref=q_ref,
            dst_ref=q_slabs.at[sec],
            send_sem=q_send_sem.at[i],
            recv_sem=q_recv_sem.at[sec],
            device_id={"sec": peer},
            device_id_type=MESH,
        )
        copy.start()
        q_copies.append(copy)

    factor = score_scale / soft_cap
    loads[0].wait()
    loads[1].wait()
    loads[2].wait()
    pair_count = sq_ref.shape[0]
    length = sk_ref.shape[0] // pair_count
    short_at = lax.broadcasted_iota(jnp.int32, (8, length), 1)
    which = lax.broadcasted_iota(jnp.int32, (8, HD), 0)
    for p in range(pair_count):
        pair_id = (sec * n_seq + seq) * pair_count + p
        limit = slens_ref[pair_id // KVH]
        q_pair = sq_ref[p : p + 1, :].astype(jnp.float32)
        stacked = jnp.zeros((8, HD), jnp.float32)
        for g in range(G):
            stacked = jnp.where(which == g, q_pair[:, g * HD : (g + 1) * HD], stacked)
        raw = lax.dot_general(
            stacked.astype(jnp.bfloat16),
            sk_ref[p * length : (p + 1) * length, :],
            CONTRACT_LAST,
            preferred_element_type=jnp.float32,
        )
        weights = jnp.where(short_at < limit, jnp.exp(soft_cap * jnp.tanh(raw * factor)), 0.0)
        totals = jnp.sum(weights, axis=1, keepdims=True)
        sums = jnp.dot(
            weights.astype(jnp.bfloat16),
            sv_ref[p * length : (p + 1) * length, :],
            preferred_element_type=jnp.float32,
        )
        result = (sums / totals).astype(short_ref.dtype)
        for g in range(G):
            short_ref[p : p + 1, g * HD : (g + 1) * HD] = result[g : g + 1, :]

    loads[3].wait()
    loads[4].wait()
    for i, peer in enumerate(sec_peers):
        pltpu.make_async_remote_copy(
            src_ref=q_ref,
            dst_ref=q_slabs.at[peer],
            send_sem=q_send_sem.at[i],
            recv_sem=q_recv_sem.at[peer],
            device_id={"sec": peer},
            device_id_type=MESH,
        ).wait_recv()
    for s in range(n_sec):
        q_rows[s * slab_rows : (s + 1) * slab_rows, :] = q_slabs[s].astype(jnp.float32)

    share = w_ref.shape[0]
    heads = share // (G * HD)
    blocks = share // HD
    lane = lax.broadcasted_iota(jnp.int32, (requests, HD), 1)
    a_copies = []
    far = deep // ((n_deep + 1) // 2)
    mirrored = (1 - far) * (n_deep - 1 - deep) + far * deep
    order = []
    for t in range(n_deep - 1):
        at = t + (t - mirrored + n_deep) // n_deep
        at = (1 - far) * (n_deep - 1 - at) + far * at
        order += [2 * at, 2 * at + 1]
    order += [mate, seq]
    mask = mask_ref[...]
    for step, dest in enumerate(order):
        offset = n_seq - 1 - step
        total_block = jnp.zeros((requests, HD), jnp.float32)
        for a in range(heads):
            at = pl.multiple_of(dest * share + a * G * HD, G * HD)
            kv_at = pl.multiple_of((dest * heads + a) * HD, HD)
            q_now = jnp.concatenate(
                [q_rows[:, pl.ds(pl.multiple_of(at + g * HD, HD), HD)] for g in range(G)], axis=0
            ).astype(jnp.bfloat16)
            raw = lax.dot_general(
                q_now,
                k_ref[:, pl.ds(kv_at, HD)],
                CONTRACT_LAST,
                preferred_element_type=jnp.float32,
            )
            weights = jnp.exp(soft_cap * jnp.tanh(raw * factor)) * mask
            totals = jnp.sum(weights, axis=1, keepdims=True)
            sums = jnp.dot(
                weights.astype(jnp.bfloat16),
                v_ref[:, pl.ds(kv_at, HD)],
                preferred_element_type=jnp.float32,
            )
            for g in range(G):
                b = a * G + g
                piece = sums[g * requests : (g + 1) * requests, :]
                total = totals[g * requests : (g + 1) * requests, :]
                total_block = jnp.where(lax.rem(lane, blocks) == b, total, total_block)
                if offset:
                    part_send[step, :, b * HD : (b + 1) * HD] = piece.astype(jnp.bfloat16)
                else:
                    part_own[:, b * HD : (b + 1) * HD] = piece
        if offset:
            high = total_block.astype(jnp.bfloat16)
            low = (total_block - high.astype(jnp.float32)).astype(jnp.bfloat16)
            part_send[step, :, share : share + HD] = jnp.where(
                lane < blocks, high.astype(jnp.float32), low.astype(jnp.float32)
            ).astype(jnp.bfloat16)
            copy = pltpu.make_async_remote_copy(
                src_ref=part_send.at[step],
                dst_ref=part_recv.at[seq],
                send_sem=a_send_sem.at[step],
                recv_sem=a_recv_sem.at[seq],
                device_id={"seq": dest},
                device_id_type=MESH,
            )
            copy.start()
            a_copies.append(copy)
        else:
            part_own[:, share : share + HD] = jnp.where(lane < blocks, total_block, 0.0)

    gathered = part_own[...]
    for peer in order[:-1]:
        pltpu.make_async_remote_copy(
            src_ref=part_send.at[0],
            dst_ref=part_recv.at[peer],
            send_sem=a_send_sem.at[0],
            recv_sem=a_recv_sem.at[peer],
            device_id={"seq": seq_peers[0]},
            device_id_type=MESH,
        ).wait_recv()
        gathered = gathered + part_recv[peer].astype(jnp.float32)

    totals_part = gathered[:, share : share + HD]
    totals_part = totals_part + pltpu.roll(totals_part, HD - blocks, 1)
    repeated = jnp.where(lane < blocks, totals_part, pltpu.roll(totals_part, blocks, 1))
    high = repeated.astype(jnp.bfloat16).astype(jnp.float32)
    tail_block = jnp.where(lane < blocks, high, repeated - high)
    sec_buf[0, :, 0:share] = gathered[:, 0:share].astype(jnp.bfloat16)
    sec_buf[0, :, share : share + HD] = tail_block.astype(jnp.bfloat16)
    b_copies = []
    for i, peer in enumerate(sec_peers):
        copy = pltpu.make_async_remote_copy(
            src_ref=sec_buf.at[0],
            dst_ref=sec_buf.at[n_sec - 1 - i],
            send_sem=b_send_sem.at[i],
            recv_sem=b_recv_sem.at[n_sec - 1 - i],
            device_id={"sec": peer},
            device_id_type=MESH,
        )
        copy.start()
        b_copies.append(copy)
    sums_now = gathered[:, 0:share]
    totals_now = jnp.where(lane < blocks, totals_part, 0.0)
    loads[5].wait()
    for i in range(1, n_sec):
        pltpu.make_async_remote_copy(
            src_ref=sec_buf.at[0],
            dst_ref=sec_buf.at[i],
            send_sem=b_send_sem.at[0],
            recv_sem=b_recv_sem.at[i],
            device_id={"sec": sec_peers[0]},
            device_id_type=MESH,
        ).wait_recv()
        arrived = sec_buf[i].astype(jnp.float32)
        sums_now = sums_now + arrived[:, 0:share]
        totals_now = totals_now + arrived[:, share : share + HD]
    totals_now = totals_now + pltpu.roll(totals_now, HD - blocks, 1)
    attention = jnp.concatenate(
        [sums_now[:, b * HD : (b + 1) * HD] / totals_now[:, b : b + 1] for b in range(blocks)],
        axis=1,
    ).astype(jnp.bfloat16)
    partial = jnp.dot(attention, w_ref[...], preferred_element_type=jnp.float32)

    rows = requests // 2
    upper, lower = partial[:rows, :], partial[rows:, :]
    first = core == 0
    pair_send[...] = jnp.where(first, lower, upper).astype(jnp.bfloat16)
    c_copy = pltpu.make_async_remote_copy(
        src_ref=pair_send,
        dst_ref=pair_recv,
        send_sem=c_send_sem,
        recv_sem=c_recv_sem,
        device_id={"seq": mate},
        device_id_type=MESH,
    )
    c_copy.start()
    mine = jnp.where(first, upper, lower)
    resid = resid_ref[...].astype(jnp.float32)
    resid = jnp.where(first, resid[:rows, :], resid[rows:, :])
    c_copy.wait_recv()
    z_buf[deep] = (mine + pair_recv[...].astype(jnp.float32)).astype(jnp.bfloat16)
    z_copies = []
    for i in range(1, n_deep):
        peer = lax.rem(deep + i, n_deep)
        copy = pltpu.make_async_remote_copy(
            src_ref=z_buf.at[deep],
            dst_ref=z_buf.at[deep],
            send_sem=z_send_sem.at[i - 1],
            recv_sem=z_recv_sem.at[deep],
            device_id={"seq": peer * 2 + core},
            device_id_type=MESH,
        )
        copy.start()
        z_copies.append(copy)
    for i in range(1, n_deep):
        peer = lax.rem(deep + i, n_deep)
        pltpu.make_async_remote_copy(
            src_ref=z_buf.at[peer],
            dst_ref=z_buf.at[peer],
            send_sem=z_send_sem.at[i - 1],
            recv_sem=z_recv_sem.at[peer],
            device_id={"seq": peer * 2 + core},
            device_id_type=MESH,
        ).wait_recv()
    for i in range(n_deep):
        resid = resid + z_buf[i].astype(jnp.float32)
    fin_buf[core] = resid.astype(jnp.bfloat16)
    f_copy = pltpu.make_async_remote_copy(
        src_ref=fin_buf.at[core],
        dst_ref=fin_buf.at[core],
        send_sem=f_send_sem,
        recv_sem=f_recv_sem,
        device_id={"seq": mate},
        device_id_type=MESH,
    )
    f_copy.start()
    for copy in q_copies + a_copies + b_copies + [c_copy] + z_copies:
        copy.wait_send()
    f_copy.wait()
    for i in range(2):
        long_ref[i * rows : (i + 1) * rows, :] = fin_buf[i]


def per_device_fused(n_sec, n_seq, *args):
    (
        long_queries,
        long_keys,
        long_values,
        page_table,
        long_lengths,
        short_queries,
        short_keys,
        short_values,
        short_lengths,
        out_weight,
        long_resid,
    ) = args
    page_count, page_len, kv_width = long_keys.shape
    tokens = page_count * page_len
    pair_count, length, _ = short_keys.shape
    slab, q_width = long_queries.shape
    requests = slab * n_sec
    share, columns = out_weight.shape
    rows = requests // 2
    packed = share + HD
    bf16, f32 = jnp.bfloat16, jnp.float32
    vmem = pl.BlockSpec(memory_space=pltpu.VMEM)
    smem = pl.BlockSpec(memory_space=pltpu.SMEM)
    hbm = pl.BlockSpec(memory_space=pltpu.HBM)
    dma = pltpu.SemaphoreType.DMA
    return pl.pallas_call(
        functools.partial(decode_kernel, n_sec, n_seq, page_len),
        out_shape=(
            pltpu.VMEM(long_resid.shape, bf16),
            pltpu.VMEM(short_queries.shape, bf16),
        ),
        in_specs=[vmem, hbm, hbm, vmem, smem, vmem, hbm, hbm, smem, hbm, vmem],
        out_specs=(vmem, vmem),
        scratch_shapes=[
            pltpu.VMEM((tokens, kv_width), bf16),
            pltpu.VMEM((tokens, kv_width), bf16),
            pltpu.VMEM((pair_count * length, HD), bf16),
            pltpu.VMEM((pair_count * length, HD), bf16),
            pltpu.VMEM((share, columns), bf16),
            pltpu.VMEM((n_sec, slab, q_width), bf16),
            pltpu.VMEM((requests, q_width), f32),
            pltpu.VMEM((G * requests, tokens), f32),
            pltpu.VMEM((n_seq, requests, packed), bf16),
            pltpu.VMEM((n_seq, requests, packed), bf16),
            pltpu.VMEM((requests, packed), f32),
            pltpu.VMEM((n_sec, requests, packed), bf16),
            pltpu.VMEM((rows, columns), bf16),
            pltpu.VMEM((rows, columns), bf16),
            pltpu.VMEM((n_seq // 2, rows, columns), bf16),
            pltpu.VMEM((2, rows, columns), bf16),
            dma((6,)),
            dma((n_sec,)),
            dma((n_sec,)),
            dma((n_seq,)),
            dma((n_seq,)),
            dma((n_sec,)),
            dma((n_sec,)),
            dma,
            dma,
            dma((n_seq // 2,)),
            dma((n_seq // 2,)),
            dma,
            dma,
        ],
        compiler_params=pltpu.CompilerParams(collective_id=0, has_side_effects=True),
    )(
        long_queries,
        long_keys.reshape(tokens, kv_width),
        long_values.reshape(tokens, kv_width),
        page_table,
        long_lengths,
        short_queries,
        short_keys.reshape(pair_count * length, HD),
        short_values.reshape(pair_count * length, HD),
        short_lengths,
        out_weight,
        long_resid,
    )


def pick_body(n_sec, n_seq, *args):
    share = args[9].shape[0]
    requests = args[0].shape[0] * n_sec
    if share % (G * HD) == 0 and n_seq % 2 == 0 and requests % 16 == 0:
        return per_device_fused(n_sec, n_seq, *args)
    return per_device(*args)


def solution(mesh):
    in_specs = (
        P("sec", None),
        P(("sec", "seq"), None, None),
        P(("sec", "seq"), None, None),
        P(),
        P(),
        P(("sec", "seq"), None),
        P(("sec", "seq"), None, None),
        P(("sec", "seq"), None, None),
        P(),
        P("seq", "sec"),
        P(None, "sec"),
    )
    out_specs = (P(None, "sec"), P(("sec", "seq"), None))
    body = functools.partial(pick_body, mesh.shape["sec"], mesh.shape["seq"])
    return jax.shard_map(
        body, mesh=mesh, in_specs=in_specs, out_specs=out_specs, check_vma=False
    )
```

```python
import functools
import jax
import jax.numpy as jnp
from jax import lax
from jax.experimental import pallas as pl
from jax.experimental.pallas import tpu as pltpu
from jax.sharding import PartitionSpec as P

KVH = 16
HD = 128
G = 2


soft_cap = 50.0
score_scale = 144.0 ** (-0.5)


def capped_weights(raw_scores, live_mask):
    capped = soft_cap * jnp.tanh(raw_scores * (score_scale / soft_cap))
    return jnp.where(live_mask, jnp.exp(capped), 0.0)


def per_device(
    long_queries,
    long_keys,
    long_values,
    page_table,
    long_lengths,
    short_queries,
    short_keys,
    short_values,
    short_lengths,
    out_weight,
    long_resid,
):
    queries = lax.all_gather(long_queries, "sec", axis=0, tiled=True)
    requests = queries.shape[0]
    page_count, page_len, kv_width = long_keys.shape
    tokens = page_count * page_len
    head_count = KVH * G
    first_page = lax.axis_index(("sec", "seq")) * page_count
    page_ids = first_page + jnp.arange(page_count, dtype=jnp.int32)
    matched = page_table[:, :, None] == page_ids[None, None, :]
    page_held = jnp.any(matched, axis=1)
    slot_index = jnp.arange(page_table.shape[1], dtype=jnp.int32)
    slot_of = jnp.sum(jnp.where(matched, slot_index[None, :, None], 0), axis=1)
    position = slot_of[:, :, None] * page_len + jnp.arange(page_len, dtype=jnp.int32)[None, None, :]
    live_mask = page_held[:, :, None] & (position < long_lengths[:, None, None])
    live_mask = live_mask.reshape(requests, tokens)
    grouped = (
        queries.reshape(requests, KVH, G, HD).transpose(1, 0, 2, 3).reshape(KVH, requests * G, HD)
    )
    key_rows = long_keys.reshape(tokens, KVH, HD)
    value_rows = long_values.reshape(tokens, KVH, HD)
    raw_scores = jnp.einsum("hqd,thd->hqt", grouped, key_rows, preferred_element_type=jnp.float32)
    token_mask = jnp.broadcast_to(live_mask[None, :, None, :], (KVH, requests, G, tokens)).reshape(
        KVH, requests * G, tokens
    )
    weights = capped_weights(raw_scores, token_mask)
    totals = jnp.sum(weights, axis=2)
    part_sums = jnp.einsum(
        "hqt,thd->hqd", weights.astype(jnp.bfloat16), value_rows, preferred_element_type=jnp.float32
    )
    part_sums = (
        part_sums.reshape(KVH, requests, G, HD)
        .transpose(1, 0, 2, 3)
        .reshape(requests, head_count * HD)
    )
    totals = totals.reshape(KVH, requests, G).transpose(1, 0, 2).reshape(requests, head_count)
    share_width = out_weight.shape[0]
    share_start = lax.axis_index("seq") * share_width
    part_sums, totals = lax.psum((part_sums, totals), ("sec", "seq"))
    attention = (
        (part_sums.reshape(requests, head_count, HD) / totals[:, :, None])
        .astype(jnp.bfloat16)
        .reshape(requests, head_count * HD)
    )
    feature_rows = lax.dynamic_slice_in_dim(attention, share_start, share_width, 1)
    partial_proj = jnp.dot(feature_rows, out_weight, preferred_element_type=jnp.float32)
    projected = lax.psum(partial_proj, "seq")
    long_out = (long_resid.astype(jnp.float32) + projected).astype(jnp.bfloat16)
    pair_count = short_queries.shape[0]
    length = short_keys.shape[1]
    pair_ids = lax.axis_index(("sec", "seq")) * pair_count + jnp.arange(pair_count, dtype=jnp.int32)
    request_of = pair_ids // KVH
    chosen = request_of[:, None] == jnp.arange(short_lengths.shape[0], dtype=jnp.int32)[None, :]
    pair_limit = jnp.sum(jnp.where(chosen, short_lengths[None, :], 0), axis=1)
    short_live = jnp.arange(length, dtype=jnp.int32)[None, :] < pair_limit[:, None]
    pair_queries = short_queries.reshape(pair_count, G, HD)
    short_scores = jnp.einsum(
        "pgd,ptd->pgt", pair_queries, short_keys, preferred_element_type=jnp.float32
    )
    short_weights = capped_weights(short_scores, short_live[:, None, :])
    short_totals = jnp.sum(short_weights, axis=2)
    short_sums = jnp.einsum(
        "pgt,ptd->pgd",
        short_weights.astype(jnp.bfloat16),
        short_values,
        preferred_element_type=jnp.float32,
    )
    short_out = (
        (short_sums / short_totals[:, :, None]).astype(jnp.bfloat16).reshape(pair_count, G * HD)
    )
    return (long_out, short_out)


MESH = pl.DeviceIdType.MESH
CONTRACT_LAST = (((1,), (1,)), ((), ()))


def decode_kernel(
    n_sec,
    n_seq,
    page_len,
    q_hbm,
    k_hbm,
    v_hbm,
    table_hbm,
    lens_hbm,
    sq_hbm,
    sk_hbm,
    sv_hbm,
    slens_hbm,
    w_hbm,
    resid_hbm,
    long_ref,
    short_ref,
    table_ref,
    lens_ref,
    sq_ref,
    slens_ref,
    resid_ref,
    k_ref,
    v_ref,
    sk_ref,
    sv_ref,
    w_ref,
    q_slabs,
    q_rows,
    mask_ref,
    part_send,
    part_recv,
    part_own,
    sec_buf,
    pair_send,
    pair_recv,
    z_buf,
    fin_buf,
    load_sem,
    q_send_sem,
    q_recv_sem,
    a_send_sem,
    a_recv_sem,
    b_send_sem,
    b_recv_sem,
    c_send_sem,
    c_recv_sem,
    z_send_sem,
    z_recv_sem,
    f_send_sem,
    f_recv_sem,
):
    sec = lax.axis_index("sec")
    seq = lax.axis_index("seq")
    core = lax.rem(seq, 2)
    deep = seq // 2
    n_deep = n_seq // 2
    mate = seq + 1 - 2 * core
    sec_peers = [lax.rem(sec + i, n_sec) for i in range(1, n_sec)]
    seq_peers = [lax.rem(seq + i, n_seq) for i in range(1, n_seq)]

    barrier = pltpu.get_barrier_semaphore()
    for peer in sec_peers:
        pl.semaphore_signal(barrier, inc=1, device_id={"sec": peer}, device_id_type=MESH)
    for peer in seq_peers:
        pl.semaphore_signal(barrier, inc=1, device_id={"seq": peer}, device_id_type=MESH)

    loads = []
    for i, (src, dst) in enumerate(
        (
            (q_hbm, q_slabs.at[sec]),
            (table_hbm, table_ref),
            (lens_hbm, lens_ref),
            (sq_hbm, sq_ref),
            (slens_hbm, slens_ref),
            (sk_hbm, sk_ref),
            (sv_hbm, sv_ref),
            (k_hbm, k_ref),
            (v_hbm, v_ref),
            (w_hbm, w_ref),
            (resid_hbm, resid_ref),
        )
    ):
        copy = pltpu.make_async_copy(src, dst, load_sem.at[i])
        copy.start()
        loads.append(copy)

    slab_rows = q_hbm.shape[0]
    requests, slots = table_ref.shape
    tokens = k_ref.shape[0]
    page_count = tokens // page_len
    first_page = (sec * n_seq + seq) * page_count
    token = lax.broadcasted_iota(jnp.int32, (requests, tokens), 1)
    row = lax.broadcasted_iota(jnp.int32, (requests, tokens), 0)
    page_of = first_page + token // page_len
    slot_of = jnp.full((requests, tokens), 1 << 20, jnp.int32)
    loads[1].wait()
    loads[2].wait()
    table = table_ref[...]
    for s in range(slots):
        slot_of = jnp.where(table[:, s : s + 1] == page_of, s, slot_of)
    limits = jnp.zeros((requests, tokens), jnp.int32)
    for r in range(requests):
        limits = jnp.where(row == r, lens_ref[r], limits)
    position = slot_of * page_len + lax.rem(token, page_len)
    live = jnp.where(position < limits, 1.0, 0.0).astype(jnp.float32)
    for g in range(G):
        mask_ref[g * requests : (g + 1) * requests, :] = live

    loads[0].wait()
    pl.semaphore_wait(barrier, n_sec + n_seq - 2)
    q_copies = []
    for i, peer in enumerate(sec_peers):
        copy = pltpu.make_async_remote_copy(
            src_ref=q_slabs.at[sec],
            dst_ref=q_slabs.at[sec],
            send_sem=q_send_sem.at[i],
            recv_sem=q_recv_sem.at[sec],
            device_id={"sec": peer},
            device_id_type=MESH,
        )
        copy.start()
        q_copies.append(copy)

    factor = score_scale / soft_cap
    for i in range(3, 7):
        loads[i].wait()
    pair_count = sq_ref.shape[0]
    length = sk_ref.shape[0] // pair_count
    short_at = lax.broadcasted_iota(jnp.int32, (8, length), 1)
    which = lax.broadcasted_iota(jnp.int32, (8, HD), 0)
    for p in range(pair_count):
        pair_id = (sec * n_seq + seq) * pair_count + p
        limit = slens_ref[pair_id // KVH]
        q_pair = sq_ref[p : p + 1, :].astype(jnp.float32)
        stacked = jnp.zeros((8, HD), jnp.float32)
        for g in range(G):
            stacked = jnp.where(which == g, q_pair[:, g * HD : (g + 1) * HD], stacked)
        raw = lax.dot_general(
            stacked.astype(jnp.bfloat16),
            sk_ref[p * length : (p + 1) * length, :],
            CONTRACT_LAST,
            preferred_element_type=jnp.float32,
        )
        weights = jnp.where(short_at < limit, jnp.exp(soft_cap * jnp.tanh(raw * factor)), 0.0)
        totals = jnp.sum(weights, axis=1, keepdims=True)
        sums = jnp.dot(
            weights.astype(jnp.bfloat16),
            sv_ref[p * length : (p + 1) * length, :],
            preferred_element_type=jnp.float32,
        )
        result = (sums / totals).astype(short_ref.dtype)
        for g in range(G):
            short_ref[p : p + 1, g * HD : (g + 1) * HD] = result[g : g + 1, :]

    loads[7].wait()
    loads[8].wait()
    for i, peer in enumerate(sec_peers):
        pltpu.make_async_remote_copy(
            src_ref=q_slabs.at[sec],
            dst_ref=q_slabs.at[peer],
            send_sem=q_send_sem.at[i],
            recv_sem=q_recv_sem.at[peer],
            device_id={"sec": peer},
            device_id_type=MESH,
        ).wait_recv()
    for s in range(n_sec):
        q_rows[s * slab_rows : (s + 1) * slab_rows, :] = q_slabs[s].astype(jnp.float32)

    share = w_ref.shape[0]
    heads = share // (G * HD)
    blocks = share // HD
    lane = lax.broadcasted_iota(jnp.int32, (requests, HD), 1)
    a_copies = []
    far = deep // ((n_deep + 1) // 2)
    mirrored = (1 - far) * (n_deep - 1 - deep) + far * deep
    order = []
    for t in range(n_deep - 1):
        at = t + (t - mirrored + n_deep) // n_deep
        at = (1 - far) * (n_deep - 1 - at) + far * at
        order += [2 * at, 2 * at + 1]
    order += [mate, seq]
    mask = mask_ref[...]
    for step, dest in enumerate(order):
        offset = n_seq - 1 - step
        total_block = jnp.zeros((requests, HD), jnp.float32)
        for a in range(heads):
            at = pl.multiple_of(dest * share + a * G * HD, G * HD)
            kv_at = pl.multiple_of((dest * heads + a) * HD, HD)
            q_now = jnp.concatenate(
                [q_rows[:, pl.ds(pl.multiple_of(at + g * HD, HD), HD)] for g in range(G)], axis=0
            ).astype(jnp.bfloat16)
            raw = lax.dot_general(
                q_now,
                k_ref[:, pl.ds(kv_at, HD)],
                CONTRACT_LAST,
                preferred_element_type=jnp.float32,
            )
            weights = jnp.exp(soft_cap * jnp.tanh(raw * factor)) * mask
            totals = jnp.sum(weights, axis=1, keepdims=True)
            sums = jnp.dot(
                weights.astype(jnp.bfloat16),
                v_ref[:, pl.ds(kv_at, HD)],
                preferred_element_type=jnp.float32,
            )
            for g in range(G):
                b = a * G + g
                piece = sums[g * requests : (g + 1) * requests, :]
                total = totals[g * requests : (g + 1) * requests, :]
                total_block = jnp.where(lax.rem(lane, blocks) == b, total, total_block)
                if offset:
                    part_send[step, :, b * HD : (b + 1) * HD] = piece.astype(jnp.bfloat16)
                else:
                    part_own[:, b * HD : (b + 1) * HD] = piece
        if offset:
            high = total_block.astype(jnp.bfloat16)
            low = (total_block - high.astype(jnp.float32)).astype(jnp.bfloat16)
            part_send[step, :, share : share + HD] = jnp.where(
                lane < blocks, high.astype(jnp.float32), low.astype(jnp.float32)
            ).astype(jnp.bfloat16)
            copy = pltpu.make_async_remote_copy(
                src_ref=part_send.at[step],
                dst_ref=part_recv.at[seq],
                send_sem=a_send_sem.at[step],
                recv_sem=a_recv_sem.at[seq],
                device_id={"seq": dest},
                device_id_type=MESH,
            )
            copy.start()
            a_copies.append(copy)
        else:
            part_own[:, share : share + HD] = jnp.where(lane < blocks, total_block, 0.0)

    gathered = part_own[...]
    for peer in order[:-1]:
        pltpu.make_async_remote_copy(
            src_ref=part_send.at[0],
            dst_ref=part_recv.at[peer],
            send_sem=a_send_sem.at[0],
            recv_sem=a_recv_sem.at[peer],
            device_id={"seq": seq_peers[0]},
            device_id_type=MESH,
        ).wait_recv()
        gathered = gathered + part_recv[peer].astype(jnp.float32)

    totals_part = gathered[:, share : share + HD]
    totals_part = totals_part + pltpu.roll(totals_part, HD - blocks, 1)
    repeated = jnp.where(lane < blocks, totals_part, pltpu.roll(totals_part, blocks, 1))
    high = repeated.astype(jnp.bfloat16).astype(jnp.float32)
    tail_block = jnp.where(lane < blocks, high, repeated - high)
    sec_buf[0, :, 0:share] = gathered[:, 0:share].astype(jnp.bfloat16)
    sec_buf[0, :, share : share + HD] = tail_block.astype(jnp.bfloat16)
    b_copies = []
    for i, peer in enumerate(sec_peers):
        copy = pltpu.make_async_remote_copy(
            src_ref=sec_buf.at[0],
            dst_ref=sec_buf.at[n_sec - 1 - i],
            send_sem=b_send_sem.at[i],
            recv_sem=b_recv_sem.at[n_sec - 1 - i],
            device_id={"sec": peer},
            device_id_type=MESH,
        )
        copy.start()
        b_copies.append(copy)
    sums_now = gathered[:, 0:share]
    totals_now = jnp.where(lane < blocks, totals_part, 0.0)
    loads[9].wait()
    loads[10].wait()
    for i in range(1, n_sec):
        pltpu.make_async_remote_copy(
            src_ref=sec_buf.at[0],
            dst_ref=sec_buf.at[i],
            send_sem=b_send_sem.at[0],
            recv_sem=b_recv_sem.at[i],
            device_id={"sec": sec_peers[0]},
            device_id_type=MESH,
        ).wait_recv()
        arrived = sec_buf[i].astype(jnp.float32)
        sums_now = sums_now + arrived[:, 0:share]
        totals_now = totals_now + arrived[:, share : share + HD]
    totals_now = totals_now + pltpu.roll(totals_now, HD - blocks, 1)
    attention = jnp.concatenate(
        [sums_now[:, b * HD : (b + 1) * HD] / totals_now[:, b : b + 1] for b in range(blocks)],
        axis=1,
    ).astype(jnp.bfloat16)
    partial = jnp.dot(attention, w_ref[...], preferred_element_type=jnp.float32)

    rows = requests // 2
    upper, lower = partial[:rows, :], partial[rows:, :]
    first = core == 0
    pair_send[...] = jnp.where(first, lower, upper).astype(jnp.bfloat16)
    c_copy = pltpu.make_async_remote_copy(
        src_ref=pair_send,
        dst_ref=pair_recv,
        send_sem=c_send_sem,
        recv_sem=c_recv_sem,
        device_id={"seq": mate},
        device_id_type=MESH,
    )
    c_copy.start()
    mine = jnp.where(first, upper, lower)
    resid = resid_ref[...].astype(jnp.float32)
    resid = jnp.where(first, resid[:rows, :], resid[rows:, :])
    c_copy.wait_recv()
    z_buf[deep] = (mine + pair_recv[...].astype(jnp.float32)).astype(jnp.bfloat16)
    z_copies = []
    for i in range(1, n_deep):
        peer = lax.rem(deep + i, n_deep)
        copy = pltpu.make_async_remote_copy(
            src_ref=z_buf.at[deep],
            dst_ref=z_buf.at[deep],
            send_sem=z_send_sem.at[i - 1],
            recv_sem=z_recv_sem.at[deep],
            device_id={"seq": peer * 2 + core},
            device_id_type=MESH,
        )
        copy.start()
        z_copies.append(copy)
    for i in range(1, n_deep):
        peer = lax.rem(deep + i, n_deep)
        pltpu.make_async_remote_copy(
            src_ref=z_buf.at[peer],
            dst_ref=z_buf.at[peer],
            send_sem=z_send_sem.at[i - 1],
            recv_sem=z_recv_sem.at[peer],
            device_id={"seq": peer * 2 + core},
            device_id_type=MESH,
        ).wait_recv()
    for i in range(n_deep):
        resid = resid + z_buf[i].astype(jnp.float32)
    fin_buf[core] = resid.astype(jnp.bfloat16)
    f_copy = pltpu.make_async_remote_copy(
        src_ref=fin_buf.at[core],
        dst_ref=fin_buf.at[core],
        send_sem=f_send_sem,
        recv_sem=f_recv_sem,
        device_id={"seq": mate},
        device_id_type=MESH,
    )
    f_copy.start()
    for copy in q_copies + a_copies + b_copies + [c_copy] + z_copies:
        copy.wait_send()
    f_copy.wait()
    for i in range(2):
        long_ref[i * rows : (i + 1) * rows, :] = fin_buf[i]


def per_device_fused(n_sec, n_seq, *args):
    (
        long_queries,
        long_keys,
        long_values,
        page_table,
        long_lengths,
        short_queries,
        short_keys,
        short_values,
        short_lengths,
        out_weight,
        long_resid,
    ) = args
    page_count, page_len, kv_width = long_keys.shape
    tokens = page_count * page_len
    pair_count, length, _ = short_keys.shape
    slab, q_width = long_queries.shape
    requests = slab * n_sec
    share, columns = out_weight.shape
    rows = requests // 2
    packed = share + HD
    bf16, f32 = jnp.bfloat16, jnp.float32
    vmem = pl.BlockSpec(memory_space=pltpu.VMEM)
    hbm = pl.BlockSpec(memory_space=pltpu.HBM)
    dma = pltpu.SemaphoreType.DMA
    return pl.pallas_call(
        functools.partial(decode_kernel, n_sec, n_seq, page_len),
        out_shape=(
            pltpu.VMEM(long_resid.shape, bf16),
            pltpu.VMEM(short_queries.shape, bf16),
        ),
        in_specs=[hbm] * 11,
        out_specs=(vmem, vmem),
        scratch_shapes=[
            pltpu.VMEM(page_table.shape, jnp.int32),
            pltpu.SMEM(long_lengths.shape, jnp.int32),
            pltpu.VMEM(short_queries.shape, bf16),
            pltpu.SMEM(short_lengths.shape, jnp.int32),
            pltpu.VMEM(long_resid.shape, bf16),
            pltpu.VMEM((tokens, kv_width), bf16),
            pltpu.VMEM((tokens, kv_width), bf16),
            pltpu.VMEM((pair_count * length, HD), bf16),
            pltpu.VMEM((pair_count * length, HD), bf16),
            pltpu.VMEM((share, columns), bf16),
            pltpu.VMEM((n_sec, slab, q_width), bf16),
            pltpu.VMEM((requests, q_width), f32),
            pltpu.VMEM((G * requests, tokens), f32),
            pltpu.VMEM((n_seq, requests, packed), bf16),
            pltpu.VMEM((n_seq, requests, packed), bf16),
            pltpu.VMEM((requests, packed), f32),
            pltpu.VMEM((n_sec, requests, packed), bf16),
            pltpu.VMEM((rows, columns), bf16),
            pltpu.VMEM((rows, columns), bf16),
            pltpu.VMEM((n_seq // 2, rows, columns), bf16),
            pltpu.VMEM((2, rows, columns), bf16),
            dma((11,)),
            dma((n_sec,)),
            dma((n_sec,)),
            dma((n_seq,)),
            dma((n_seq,)),
            dma((n_sec,)),
            dma((n_sec,)),
            dma,
            dma,
            dma((n_seq // 2,)),
            dma((n_seq // 2,)),
            dma,
            dma,
        ],
        compiler_params=pltpu.CompilerParams(collective_id=0, has_side_effects=True),
    )(
        long_queries,
        long_keys.reshape(tokens, kv_width),
        long_values.reshape(tokens, kv_width),
        page_table,
        long_lengths,
        short_queries,
        short_keys.reshape(pair_count * length, HD),
        short_values.reshape(pair_count * length, HD),
        short_lengths,
        out_weight,
        long_resid,
    )


def pick_body(n_sec, n_seq, *args):
    share = args[9].shape[0]
    requests = args[0].shape[0] * n_sec
    if share % (G * HD) == 0 and n_seq % 2 == 0 and requests % 16 == 0:
        return per_device_fused(n_sec, n_seq, *args)
    return per_device(*args)


def solution(mesh):
    in_specs = (
        P("sec", None),
        P(("sec", "seq"), None, None),
        P(("sec", "seq"), None, None),
        P(),
        P(),
        P(("sec", "seq"), None),
        P(("sec", "seq"), None, None),
        P(("sec", "seq"), None, None),
        P(),
        P("seq", "sec"),
        P(None, "sec"),
    )
    out_specs = (P(None, "sec"), P(("sec", "seq"), None))
    body = functools.partial(pick_body, mesh.shape["sec"], mesh.shape["seq"])
    return jax.shard_map(
        body, mesh=mesh, in_specs=in_specs, out_specs=out_specs, check_vma=False
    )
```
